128 devices in a mesh: group: 2 (over z_lo), shard: 32 (over x, y, core), tensor: 2 (over z_hi).
Axes of the slice: x: 4, y: 4, z: 4 (z_hi: 2, z_lo: 2; z = z_hi * 2 + z_lo), core: 2. Of those that a mesh axis runs over, the one named last changes fastest.
Arguments:
- down_anchor: float32 [8192, 4096], P('shard', 'tensor'), may hold values from -6 to 6
- down_local: float32 [2, 8192, 4096], P('group', 'shard', 'tensor'), may hold values from -6 to 6
- down_moment: float32 [8192, 4096], P(('shard', 'group'), 'tensor'), may hold values from -4 to 4
- norm_anchor: float32 [2, 4096], P(None, ('shard', 'tensor')), may hold values from 0.5 to 1.5
- norm_local: float32 [2, 2, 4096], P('group', None, ('shard', 'tensor')), may hold values from 0.1 to 1.9
- norm_moment: float32 [2, 4096], P('group', ('shard', 'tensor')), may hold values from -4 to 4
- gate_anchor: float32 [8192, 4096], P('tensor', 'shard'), may hold values from -6 to 6
- gate_local: float32 [2, 8192, 4096], P('group', 'tensor', 'shard'), may hold values from -6 to 6
- gate_moment: float32 [8192, 4096], P('tensor', 'shard'), may hold values from -4 to 4
- factor_basis: float32 [64, 4096], P(None, 'shard'), may hold values from -0.09375 to 0.09375
Outputs:
- new_down_anchor: float32 [8192, 4096], P('shard', 'tensor')
- new_down_moment: float32 [8192, 4096], P(('shard', 'group'), 'tensor')
- new_norm_anchor: float32 [2, 4096], P(None, ('shard', 'tensor'))
- new_norm_moment: float32 [2, 4096], P('group', ('shard', 'tensor'))
- new_gate_anchor: float32 [8192, 4096], P('tensor', 'shard')
- new_gate_moment: float32 [8192, 4096], P('tensor', 'shard')
The draws below stay inside these ranges and needn't reach their ends.
All inputs are finite; a program needn't handle non-finite values.
Results may differ from the reference program's by a relative error of at most 0.000096.
Values sent between devices are 32-bit elements; how exact they have to be, the bound alone decides.
A program may use at most 64 MiB of HBM per device.

```python
import jax
import jax.numpy as jnp
from jax import lax

D = 4096
FF = 8192
RANK = 64
NORMS = 2
G = 2


def block_levels(rng, extent, pieces, low, largest):
    def one(position, parts):
        steps = jax.random.uniform(jax.random.fold_in(jax.random.fold_in(rng, 6), position), (parts,), jnp.float32, low / len(pieces), largest / len(pieces))
        return jnp.repeat(jnp.exp(steps), extent[position] // parts).reshape((-1,) + (1,) * (len(extent) - position - 1))

    loudness = one(*pieces[0])
    for cut in pieces[1:]:
        loudness = loudness * one(*cut)
    return loudness


def normal_values(stream_key, dims, scale, limit, pieces=(), kind=jnp.bfloat16):
    factor_of = block_levels(stream_key, dims, pieces, -0.22, 0.18) if pieces else 1.0
    result = jax.random.normal(stream_key, dims, jnp.float32) * scale * factor_of
    return jnp.minimum(jnp.maximum(result, -limit), limit).astype(kind)


def setup_inputs(seed: int = 0) -> dict:
    keys = jax.random.split(jax.random.key(seed), 11)
    down_anchor = normal_values(keys[0], (FF, D), 1.0, 6.0, ((0, 32), (1, 2)), jnp.float32)
    down_local = normal_values(keys[1], (G, FF, D), 1.0, 6.0, ((0, 2), (1, 32), (2, 2)), jnp.float32)
    down_moment = normal_values(keys[2], (FF, D), 0.5, 4.0, ((0, 64), (1, 2)), jnp.float32)
    norm_anchor = jnp.clip(1.0 + 0.1 * jax.random.normal(keys[3], (NORMS, D), jnp.float32), 0.5, 1.5)
    norm_local = jnp.clip(1.0 + 0.18 * jax.random.normal(keys[4], (G, NORMS, D), jnp.float32), 0.1, 1.9)
    norm_moment = normal_values(keys[5], (NORMS, D), 0.5, 4.0, ((0, 2), (1, 64)), jnp.float32)
    gate_anchor = normal_values(keys[6], (FF, D), 1.0, 6.0, ((0, 2), (1, 32)), jnp.float32)
    gate_local = normal_values(keys[7], (G, FF, D), 1.0, 6.0, ((0, 2), (1, 2), (2, 32)), jnp.float32)
    gate_moment = normal_values(keys[8], (FF, D), 0.5, 4.0, ((0, 2), (1, 32)), jnp.float32)
    factor_basis = normal_values(keys[9], (RANK, D), D ** -0.5, 0.09375, ((1, 32),), jnp.float32)
    return dict(down_anchor=down_anchor, down_local=down_local, down_moment=down_moment, norm_anchor=norm_anchor, norm_local=norm_local, norm_moment=norm_moment, gate_anchor=gate_anchor, gate_local=gate_local, gate_moment=gate_moment, factor_basis=factor_basis)


outer_rate = 0.7
momentum = 0.9


def advance(anchor, moment, delta):
    moment_next = momentum * moment + delta
    anchor_next = anchor - outer_rate * (delta + momentum * moment_next)
    return anchor_next, moment_next


def reference(down_anchor, down_local, down_moment, norm_anchor, norm_local, norm_moment, gate_anchor, gate_local, gate_moment, factor_basis):
    groups = down_local.shape[0]
    down_delta = jnp.sum(down_anchor[None] - down_local, axis=0) / groups
    norm_delta = jnp.sum(norm_anchor[None] - norm_local, axis=0) / groups
    summed = jnp.sum(gate_anchor[None] - gate_local, axis=0)
    factors = jnp.dot(factor_basis, summed.T, precision=lax.Precision.HIGHEST) / groups
    gate_delta = jnp.dot(factors.T, factor_basis, precision=lax.Precision.HIGHEST)
    new_down_anchor, new_down_moment = advance(down_anchor, down_moment, down_delta)
    new_norm_anchor, new_norm_moment = advance(norm_anchor, norm_moment, norm_delta)
    new_gate_anchor, new_gate_moment = advance(gate_anchor, gate_moment, gate_delta)
    return (new_down_anchor, new_down_moment, new_norm_anchor, new_norm_moment, new_gate_anchor, new_gate_moment)
```

```python
import jax
import jax.numpy as jnp
from jax import lax
from jax.experimental import pallas as pl
from jax.experimental.pallas import tpu as pltpu
from jax.sharding import PartitionSpec as P

outer_rate = 0.7
momentum = 0.9
groups = 2

local_weight = outer_rate * (1.0 + momentum) / groups
moment_weight = outer_rate * momentum * momentum
anchor_weight = 1.0 - outer_rate * (1.0 + momentum)

SIDE = 4
HIGHEST = lax.Precision.HIGHEST
MESH = pl.DeviceIdType.MESH


def kernel(
    down_anchor,
    down_local,
    down_moment,
    norm_anchor,
    norm_local,
    norm_moment,
    gate_anchor,
    gate_local,
    gate_moment,
    factor_basis,
    new_down_anchor,
    new_down_moment,
    new_norm_anchor,
    new_norm_moment,
    new_gate_anchor,
    new_gate_moment,
    da,
    dl,
    dm,
    part,
    peer_local,
    peer_part,
    nl,
    nm,
    ga,
    gl,
    gm,
    basis,
    away,
    home,
    from_core,
    from_x,
    row,
    from_y,
    piece,
    from_z,
    whole,
    load_sem,
    store_sem,
    down_send,
    down_recv,
    part_send,
    part_recv,
    norm_send,
    norm_recv,
    core_send,
    core_recv,
    x_send,
    x_recv,
    y_send,
    y_recv,
    z_send,
    z_recv,
):
    g = lax.axis_index("group")
    s = lax.axis_index("shard")
    x, y, core = s // (2 * SIDE), (s // 2) % SIDE, s % 2
    half = da.shape[0] // 2
    wide = gl.shape[0] // 2
    span = wide // SIDE
    tall = piece.shape[0]
    chunks = part_send.shape[0]
    step = half // chunks

    other_group = {"group": 1 - g}
    other_core = {"shard": s + 1 - 2 * core}

    def along_x(d):
        return {"shard": ((x + d) % SIDE) * 2 * SIDE + y * 2 + core}

    def along_y(d):
        return {"shard": x * 2 * SIDE + ((y + d) % SIDE) * 2 + core}

    def remote(src, dst, send, recv, device):
        return pltpu.make_async_remote_copy(
            src_ref=src, dst_ref=dst, send_sem=send, recv_sem=recv, device_id=device, device_id_type=MESH
        )

    barrier = pltpu.get_barrier_semaphore()
    partners = [other_group, other_core]
    partners += [along_x(d) for d in range(1, SIDE)] + [along_y(d) for d in range(1, SIDE)]
    for device in partners:
        pl.semaphore_signal(barrier, inc=1, device_id=device, device_id_type=MESH)

    mine = pl.ds(pl.multiple_of(g * half, half), half)
    theirs = pl.ds(pl.multiple_of((1 - g) * half, half), half)
    near = pl.ds(pl.multiple_of(core * wide, wide), wide)
    far = pl.ds(pl.multiple_of((1 - core) * wide, wide), wide)

    pairs = [
        (factor_basis, basis),
        (gate_anchor.at[far], ga.at[far]),
        (gate_local.at[0, far], gl.at[far]),
        (gate_anchor.at[near], ga.at[near]),
        (gate_local.at[0, near], gl.at[near]),
        (down_local.at[0, mine], dl.at[mine]),
        (down_moment, dm),
        (gate_moment, gm),
        (down_anchor, da),
        (down_local.at[0, theirs], dl.at[theirs]),
    ]
    loads = [pltpu.make_async_copy(src, dst, load_sem.at[i]) for i, (src, dst) in enumerate(pairs)]
    for load in loads:
        load.start()

    pl.semaphore_wait(barrier, len(partners))

    norm_copies = [
        remote(norm_local, nl, norm_send.at[0], norm_recv.at[0], other_group),
        remote(norm_moment, nm, norm_send.at[1], norm_recv.at[1], other_group),
    ]
    for copy in norm_copies:
        copy.start()
    local_copy = remote(down_local.at[0, theirs], peer_local, down_send, down_recv, other_group)
    local_copy.start()

    def factor(start, out):
        def block(i, carry):
            rows = pl.ds(pl.multiple_of(start + i * span, span), span)
            diff = ga[rows, :] - gl[rows, :]
            out[i] = lax.dot_general(
                basis[...], diff, (((1,), (1,)), ((), ())), precision=HIGHEST, preferred_element_type=jnp.float32
            )
            return carry

        lax.fori_loop(0, SIDE, block, 0)

    for load in loads[:3]:
        load.wait()
    factor((1 - core) * wide, away)
    core_copy = remote(away, from_core, core_send.at[0], core_recv.at[0], other_core)
    core_copy.start()
    for load in loads[3:5]:
        load.wait()
    factor(core * wide, home)

    for load in loads[5:7]:
        load.wait()

    def combine(i, carry):
        rows = pl.ds(pl.multiple_of(i * 16, 16), 16)
        own = pl.ds(pl.multiple_of(g * half + i * 16, 16), 16)
        part[rows, :] = local_weight * dl[own, :] - moment_weight * dm[rows, :]
        return carry

    lax.fori_loop(0, half // 16, combine, 0)

    core_copy.wait_recv()
    x_copies = []
    for d in (2, 1, 3):
        to = (x + d) % SIDE
        home[to] = home[to] + from_core[to]
        x_copies.append(remote(home.at[to], from_x.at[d - 1], x_send.at[d - 1], x_recv.at[d - 1], along_x(d)))
        x_copies[-1].start()
    row[...] = home[x] + from_core[x]
    for copy in x_copies:
        copy.wait_recv()
    row[...] = (row[...] + from_x[0]) + (from_x[1] + from_x[2])

    y_copies = []
    for d in (2, 1, 3):
        rows = pl.ds(pl.multiple_of(((y + d) % SIDE) * tall, tall), tall)
        y_copies.append(remote(row.at[rows], from_y.at[d - 1], y_send.at[d - 1], y_recv.at[d - 1], along_y(d)))
        y_copies[-1].start()
    kept = pl.ds(pl.multiple_of(y * tall, tall), tall)
    for copy in y_copies:
        copy.wait_recv()
    piece[...] = (row[kept, :] + from_y[0]) + (from_y[1] + from_y[2])

    z_copy = remote(piece, from_z, z_send, z_recv, other_group)
    z_copy.start()
    part_copies = []
    for i in range(chunks):
        rows = pl.ds(i * step, step)
        part_copies.append(
            remote(part.at[rows], peer_part.at[rows], part_send.at[i], part_recv.at[i], other_group)
        )
        part_copies[-1].start()
    z_copy.wait_recv()

    slot = core * SIDE + x
    whole[slot, kept, :] = (piece[...] + from_z[...]) * (1.0 / groups)
    y_back = []
    for d in (2, 1, 3):
        here = whole.at[slot, kept]
        y_back.append(remote(here, here, y_send.at[d + 2], y_recv.at[d + 2], along_y(d)))
        y_back[-1].start()
    for copy in y_back:
        copy.wait_recv()
    x_back = []
    for d in (2, 1, 3):
        here = whole.at[slot]
        x_back.append(remote(here, here, x_send.at[d + 2], x_recv.at[d + 2], along_x(d)))
        x_back[-1].start()
    for copy in x_back:
        copy.wait_recv()
    ours = whole.at[pl.ds(pl.multiple_of(core * SIDE, SIDE), SIDE)]
    core_back = remote(ours, ours, core_send.at[1], core_recv.at[1], other_core)
    core_back.start()

    loads[7].wait()

    def rebuild(first):
        def block(i, carry):
            rows = pl.ds(pl.multiple_of((first + i) * span, span), span)
            delta = lax.dot_general(
                whole[first + i], basis[...], (((0,), (0,)), ((), ())), precision=HIGHEST,
                preferred_element_type=jnp.float32,
            )
            moment = momentum * gm[rows, :] + delta
            gm[rows, :] = moment
            ga[rows, :] = ga[rows, :] - outer_rate * (delta + momentum * moment)
            return carry

        lax.fori_loop(0, SIDE, block, 0)

    rebuild(core * SIDE)
    core_back.wait_recv()
    rebuild((1 - core) * SIDE)
    stores = [
        pltpu.make_async_copy(ga, new_gate_anchor, store_sem.at[0]),
        pltpu.make_async_copy(gm, new_gate_moment, store_sem.at[1]),
    ]
    for store in stores:
        store.start()

    for copy in norm_copies:
        copy.wait_recv()
    norm_delta = norm_anchor[...] - (norm_local[0] + nl[0]) * (1.0 / groups)
    picked = lax.broadcasted_iota(jnp.int32, norm_anchor.shape, 0) == g
    norm_next = momentum * jnp.where(picked, norm_moment[...], nm[...]) + norm_delta
    new_norm_anchor[...] = norm_anchor[...] - outer_rate * (norm_delta + momentum * norm_next)
    new_norm_moment[...] = jnp.where(g == 0, norm_next[0:1], norm_next[1:2])

    loads[8].wait()
    local_copy.wait_recv()

    def own_half(i, carry):
        rows = pl.ds(pl.multiple_of(i * 16, 16), 16)
        own = pl.ds(pl.multiple_of(g * half + i * 16, 16), 16)
        anchor = da[own, :]
        dm[rows, :] = momentum * dm[rows, :] + (anchor - (dl[own, :] + peer_local[rows, :]) * (1.0 / groups))
        da[own, :] = (anchor_weight * anchor + local_weight * peer_local[rows, :]) + part[rows, :]
        return carry

    lax.fori_loop(0, half // 16, own_half, 0)
    stores += [
        pltpu.make_async_copy(dm, new_down_moment, store_sem.at[2]),
        pltpu.make_async_copy(da.at[mine], new_down_anchor.at[mine], store_sem.at[3]),
    ]
    stores[2].start()
    stores[3].start()
    loads[9].wait()

    for c in range(chunks):
        part_copies[c].wait_recv()

        def other_half(i, carry):
            rows = pl.ds(pl.multiple_of(c * step + i * 8, 8), 8)
            far_rows = pl.ds(pl.multiple_of((1 - g) * half + c * step + i * 8, 8), 8)
            da[far_rows, :] = (
                anchor_weight * da[far_rows, :] + local_weight * dl[far_rows, :]
            ) + peer_part[rows, :]
            return carry

        lax.fori_loop(0, step // 8, other_half, 0)
        chunk = pl.ds(pl.multiple_of((1 - g) * half + c * step, step), step)
        stores.append(pltpu.make_async_copy(da.at[chunk], new_down_anchor.at[chunk], store_sem.at[4 + c]))
        stores[-1].start()

    for copy in norm_copies + [local_copy, core_copy, z_copy, core_back]:
        copy.wait_send()
    for copy in x_copies + y_copies + part_copies + y_back + x_back:
        copy.wait_send()
    for store in stores:
        store.wait()


def body(*args):
    down_anchor, _, down_moment, norm_anchor, norm_local, norm_moment, gate_anchor, _, _, factor_basis = args
    f32 = jnp.float32
    half, width = down_moment.shape
    rank, depth = factor_basis.shape
    hidden = gate_anchor.shape[0]
    wide = hidden // 2
    span = wide // SIDE
    tall = rank // SIDE
    chunks = 4
    anywhere = pl.BlockSpec(memory_space=pl.ANY)
    vmem = pl.BlockSpec(memory_space=pltpu.VMEM)
    dma = pltpu.SemaphoreType.DMA
    shapes = [
        pltpu.VMEM((2 * half, width), f32),
        pltpu.VMEM((2 * half, width), f32),
        pltpu.VMEM((half, width), f32),
        pltpu.VMEM((half, width), f32),
        pltpu.VMEM((half, width), f32),
        pltpu.VMEM((half, width), f32),
        pltpu.VMEM(norm_local.shape, f32),
        pltpu.VMEM(norm_moment.shape, f32),
        pltpu.VMEM((hidden, depth), f32),
        pltpu.VMEM((hidden, depth), f32),
        pltpu.VMEM((hidden, depth), f32),
        pltpu.VMEM((rank, depth), f32),
        pltpu.VMEM((SIDE, rank, span), f32),
        pltpu.VMEM((SIDE, rank, span), f32),
        pltpu.VMEM((SIDE, rank, span), f32),
        pltpu.VMEM((SIDE - 1, rank, span), f32),
        pltpu.VMEM((rank, span), f32),
        pltpu.VMEM((SIDE - 1, tall, span), f32),
        pltpu.VMEM((tall, span), f32),
        pltpu.VMEM((tall, span), f32),
        pltpu.VMEM((2 * SIDE, rank, span), f32),
        dma((10,)),
        dma((4 + chunks,)),
        dma,
        dma,
        dma((chunks,)),
        dma((chunks,)),
        dma((2,)),
        dma((2,)),
        dma((2,)),
        dma((2,)),
        dma((6,)),
        dma((6,)),
        dma((6,)),
        dma((6,)),
        dma,
        dma,
    ]
    outs = [
        jax.ShapeDtypeStruct(a.shape, f32)
        for a in (down_anchor, down_moment, norm_anchor, norm_moment, gate_anchor, gate_anchor)
    ]
    return pl.pallas_call(
        kernel,
        out_shape=outs,
        in_specs=[anywhere] * 3 + [vmem] * 3 + [anywhere] * 4,
        out_specs=[anywhere] * 2 + [vmem] * 2 + [anywhere] * 2,
        scratch_shapes=shapes,
        compiler_params=pltpu.CompilerParams(collective_id=0, has_side_effects=True),
    )(*args)


def solution(mesh):
    placed = (
        P("shard", "tensor"),
        P("group", "shard", "tensor"),
        P(("shard", "group"), "tensor"),
        P(None, ("shard", "tensor")),
        P("group", None, ("shard", "tensor")),
        P("group", ("shard", "tensor")),
        P("tensor", "shard"),
        P("group", "tensor", "shard"),
        P("tensor", "shard"),
        P(None, "shard"),
    )
    return jax.shard_map(
        body,
        mesh=mesh,
        in_specs=placed,
        out_specs=(
            P("shard", "tensor"),
            P(("shard", "group"), "tensor"),
            P(None, ("shard", "tensor")),
            P("group", ("shard", "tensor")),
            P("tensor", "shard"),
            P("tensor", "shard"),
        ),
        check_vma=False,
    )
```

```python
import jax
import jax.numpy as jnp
from jax import lax
from jax.experimental import pallas as pl
from jax.experimental.pallas import tpu as pltpu
from jax.sharding import PartitionSpec as P

outer_rate = 0.7
momentum = 0.9
groups = 2

local_weight = outer_rate * (1.0 + momentum) / groups
moment_weight = outer_rate * momentum * momentum
anchor_weight = 1.0 - outer_rate * (1.0 + momentum)

SIDE = 4
HIGHEST = lax.Precision.HIGHEST
MESH = pl.DeviceIdType.MESH


def kernel(
    down_anchor,
    down_local,
    down_moment,
    norm_anchor,
    norm_local,
    norm_moment,
    gate_anchor,
    gate_local,
    gate_moment,
    factor_basis,
    da,
    dm,
    new_norm_anchor,
    new_norm_moment,
    ga,
    gm,
    dl,
    part,
    peer_local,
    peer_part,
    nl,
    nm,
    gl,
    basis,
    away,
    home,
    from_core,
    from_x,
    row,
    from_y,
    piece,
    from_z,
    whole,
    load_sem,
    down_send,
    down_recv,
    part_send,
    part_recv,
    norm_send,
    norm_recv,
    core_send,
    core_recv,
    x_send,
    x_recv,
    y_send,
    y_recv,
    z_send,
    z_recv,
):
    g = lax.axis_index("group")
    s = lax.axis_index("shard")
    x, y, core = s // (2 * SIDE), (s // 2) % SIDE, s % 2
    half = da.shape[0] // 2
    wide = gl.shape[0] // 2
    span = wide // SIDE
    tall = piece.shape[0]
    chunks = part_send.shape[0]
    step = half // chunks

    other_group = {"group": 1 - g}
    other_core = {"shard": s + 1 - 2 * core}

    def along_x(d):
        return {"shard": ((x + d) % SIDE) * 2 * SIDE + y * 2 + core}

    def along_y(d):
        return {"shard": x * 2 * SIDE + ((y + d) % SIDE) * 2 + core}

    def remote(src, dst, send, recv, device):
        return pltpu.make_async_remote_copy(
            src_ref=src, dst_ref=dst, send_sem=send, recv_sem=recv, device_id=device, device_id_type=MESH
        )

    barrier = pltpu.get_barrier_semaphore()
    partners = [other_group, other_core]
    partners += [along_x(d) for d in range(1, SIDE)] + [along_y(d) for d in range(1, SIDE)]
    for device in partners:
        pl.semaphore_signal(barrier, inc=1, device_id=device, device_id_type=MESH)

    mine = pl.ds(pl.multiple_of(g * half, half), half)
    theirs = pl.ds(pl.multiple_of((1 - g) * half, half), half)
    near = pl.ds(pl.multiple_of(core * wide, wide), wide)
    far = pl.ds(pl.multiple_of((1 - core) * wide, wide), wide)

    pairs = [
        (factor_basis, basis),
        (gate_anchor.at[far], ga.at[far]),
        (gate_local.at[0, far], gl.at[far]),
        (gate_anchor.at[near], ga.at[near]),
        (gate_local.at[0, near], gl.at[near]),
        (down_local.at[0, mine], dl.at[mine]),
        (down_moment, dm),
        (gate_moment, gm),
        (down_anchor, da),
        (down_local.at[0, theirs], dl.at[theirs]),
    ]
    loads = [pltpu.make_async_copy(src, dst, load_sem.at[i]) for i, (src, dst) in enumerate(pairs)]
    for load in loads:
        load.start()

    pl.semaphore_wait(barrier, len(partners))

    norm_copies = [
        remote(norm_local, nl, norm_send.at[0], norm_recv.at[0], other_group),
        remote(norm_moment, nm, norm_send.at[1], norm_recv.at[1], other_group),
    ]
    for copy in norm_copies:
        copy.start()
    local_copy = remote(down_local.at[0, theirs], peer_local, down_send, down_recv, other_group)
    local_copy.start()

    def factor(start, out):
        def block(i, carry):
            rows = pl.ds(pl.multiple_of(start + i * span, span), span)
            diff = ga[rows, :] - gl[rows, :]
            out[i] = lax.dot_general(
                basis[...], diff, (((1,), (1,)), ((), ())), precision=HIGHEST, preferred_element_type=jnp.float32
            )
            return carry

        lax.fori_loop(0, SIDE, block, 0)

    for load in loads[:3]:
        load.wait()
    factor((1 - core) * wide, away)
    core_copy = remote(away, from_core, core_send.at[0], core_recv.at[0], other_core)
    core_copy.start()
    for load in loads[3:5]:
        load.wait()
    factor(core * wide, home)

    for load in loads[5:7]:
        load.wait()

    def combine(i, carry):
        rows = pl.ds(pl.multiple_of(i * 16, 16), 16)
        own = pl.ds(pl.multiple_of(g * half + i * 16, 16), 16)
        part[rows, :] = local_weight * dl[own, :] - moment_weight * dm[rows, :]
        return carry

    lax.fori_loop(0, half // 16, combine, 0)

    core_copy.wait_recv()
    x_copies = []
    for d in (2, 1, 3):
        to = (x + d) % SIDE
        home[to] = home[to] + from_core[to]
        x_copies.append(remote(home.at[to], from_x.at[d - 1], x_send.at[d - 1], x_recv.at[d - 1], along_x(d)))
        x_copies[-1].start()
    row[...] = home[x] + from_core[x]
    for copy in x_copies:
        copy.wait_recv()
    row[...] = (row[...] + from_x[0]) + (from_x[1] + from_x[2])

    y_copies = []
    for d in (2, 1, 3):
        rows = pl.ds(pl.multiple_of(((y + d) % SIDE) * tall, tall), tall)
        y_copies.append(remote(row.at[rows], from_y.at[d - 1], y_send.at[d - 1], y_recv.at[d - 1], along_y(d)))
        y_copies[-1].start()
    kept = pl.ds(pl.multiple_of(y * tall, tall), tall)
    for copy in y_copies:
        copy.wait_recv()
    piece[...] = (row[kept, :] + from_y[0]) + (from_y[1] + from_y[2])

    z_copy = remote(piece, from_z, z_send, z_recv, other_group)
    z_copy.start()
    part_copies = []
    for i in range(chunks):
        rows = pl.ds(i * step, step)
        part_copies.append(
            remote(part.at[rows], peer_part.at[rows], part_send.at[i], part_recv.at[i], other_group)
        )
        part_copies[-1].start()
    z_copy.wait_recv()

    slot = core * SIDE + x
    whole[slot, kept, :] = (piece[...] + from_z[...]) * (1.0 / groups)
    y_back = []
    for d in (2, 1, 3):
        here = whole.at[slot, kept]
        y_back.append(remote(here, here, y_send.at[d + 2], y_recv.at[d + 2], along_y(d)))
        y_back[-1].start()
    for copy in y_back:
        copy.wait_recv()
    x_back = []
    for d in (2, 1, 3):
        here = whole.at[slot]
        x_back.append(remote(here, here, x_send.at[d + 2], x_recv.at[d + 2], along_x(d)))
        x_back[-1].start()
    for copy in x_back:
        copy.wait_recv()
    ours = whole.at[pl.ds(pl.multiple_of(core * SIDE, SIDE), SIDE)]
    core_back = remote(ours, ours, core_send.at[1], core_recv.at[1], other_core)
    core_back.start()

    loads[7].wait()

    def rebuild(first):
        def block(i, carry):
            rows = pl.ds(pl.multiple_of((first + i) * span, span), span)
            delta = lax.dot_general(
                whole[first + i], basis[...], (((0,), (0,)), ((), ())), precision=HIGHEST,
                preferred_element_type=jnp.float32,
            )
            moment = momentum * gm[rows, :] + delta
            gm[rows, :] = moment
            ga[rows, :] = ga[rows, :] - outer_rate * (delta + momentum * moment)
            return carry

        lax.fori_loop(0, SIDE, block, 0)

    rebuild(core * SIDE)
    core_back.wait_recv()
    rebuild((1 - core) * SIDE)

    for copy in norm_copies:
        copy.wait_recv()
    norm_delta = norm_anchor[...] - (norm_local[0] + nl[0]) * (1.0 / groups)
    picked = lax.broadcasted_iota(jnp.int32, norm_anchor.shape, 0) == g
    norm_next = momentum * jnp.where(picked, norm_moment[...], nm[...]) + norm_delta
    new_norm_anchor[...] = norm_anchor[...] - outer_rate * (norm_delta + momentum * norm_next)
    new_norm_moment[...] = jnp.where(g == 0, norm_next[0:1], norm_next[1:2])

    loads[8].wait()
    local_copy.wait_recv()

    def own_half(i, carry):
        rows = pl.ds(pl.multiple_of(i * 16, 16), 16)
        own = pl.ds(pl.multiple_of(g * half + i * 16, 16), 16)
        anchor = da[own, :]
        dm[rows, :] = momentum * dm[rows, :] + (anchor - (dl[own, :] + peer_local[rows, :]) * (1.0 / groups))
        da[own, :] = (anchor_weight * anchor + local_weight * peer_local[rows, :]) + part[rows, :]
        return carry

    lax.fori_loop(0, half // 16, own_half, 0)
    loads[9].wait()

    for c in range(chunks):
        part_copies[c].wait_recv()

        def other_half(i, carry):
            rows = pl.ds(pl.multiple_of(c * step + i * 8, 8), 8)
            far_rows = pl.ds(pl.multiple_of((1 - g) * half + c * step + i * 8, 8), 8)
            da[far_rows, :] = (
                anchor_weight * da[far_rows, :] + local_weight * dl[far_rows, :]
            ) + peer_part[rows, :]
            return carry

        lax.fori_loop(0, step // 8, other_half, 0)

    for copy in norm_copies + [local_copy, core_copy, z_copy, core_back]:
        copy.wait_send()
    for copy in x_copies + y_copies + part_copies + y_back + x_back:
        copy.wait_send()


def write_out(*refs):
    count = len(refs) // 2
    sems = refs[-1]
    copies = [pltpu.make_async_copy(refs[i], refs[count + i], sems.at[i]) for i in (0, 1, 4, 5)]
    for copy in copies:
        copy.start()
    for i in (2, 3):
        refs[count + i][...] = refs[i][...]
    for copy in copies:
        copy.wait()


def body(*args):
    down_anchor, _, down_moment, norm_anchor, norm_local, norm_moment, gate_anchor, _, _, factor_basis = args
    f32 = jnp.float32
    half, width = down_moment.shape
    rank, depth = factor_basis.shape
    hidden = gate_anchor.shape[0]
    wide = hidden // 2
    span = wide // SIDE
    tall = rank // SIDE
    chunks = 4
    anywhere = pl.BlockSpec(memory_space=pl.ANY)
    vmem = pl.BlockSpec(memory_space=pltpu.VMEM)
    dma = pltpu.SemaphoreType.DMA
    shapes = [
        pltpu.VMEM((2 * half, width), f32),
        pltpu.VMEM((half, width), f32),
        pltpu.VMEM((half, width), f32),
        pltpu.VMEM((half, width), f32),
        pltpu.VMEM(norm_local.shape, f32),
        pltpu.VMEM(norm_moment.shape, f32),
        pltpu.VMEM((hidden, depth), f32),
        pltpu.VMEM((rank, depth), f32),
        pltpu.VMEM((SIDE, rank, span), f32),
        pltpu.VMEM((SIDE, rank, span), f32),
        pltpu.VMEM((SIDE, rank, span), f32),
        pltpu.VMEM((SIDE - 1, rank, span), f32),
        pltpu.VMEM((rank, span), f32),
        pltpu.VMEM((SIDE - 1, tall, span), f32),
        pltpu.VMEM((tall, span), f32),
        pltpu.VMEM((tall, span), f32),
        pltpu.VMEM((2 * SIDE, rank, span), f32),
        dma((10,)),
        dma,
        dma,
        dma((chunks,)),
        dma((chunks,)),
        dma((2,)),
        dma((2,)),
        dma((2,)),
        dma((2,)),
        dma((6,)),
        dma((6,)),
        dma((6,)),
        dma((6,)),
        dma,
        dma,
    ]
    held = [pltpu.VMEM(a.shape, f32) for a in (down_anchor, down_moment, norm_anchor, norm_moment, gate_anchor, gate_anchor)]
    results = pl.pallas_call(
        kernel,
        out_shape=held,
        in_specs=[anywhere] * 3 + [vmem] * 3 + [anywhere] * 4,
        out_specs=[vmem] * 6,
        scratch_shapes=shapes,
        compiler_params=pltpu.CompilerParams(collective_id=0, has_side_effects=True, vmem_limit_bytes=48 << 20),
    )(*args)
    return pl.pallas_call(
        write_out,
        out_shape=[jax.ShapeDtypeStruct(a.shape, f32) for a in held],
        in_specs=[vmem] * 6,
        out_specs=[anywhere] * 2 + [vmem] * 2 + [anywhere] * 2,
        scratch_shapes=[dma((6,))],
        compiler_params=pltpu.CompilerParams(vmem_limit_bytes=8 << 20),
    )(*results)


def solution(mesh):
    placed = (
        P("shard", "tensor"),
        P("group", "shard", "tensor"),
        P(("shard", "group"), "tensor"),
        P(None, ("shard", "tensor")),
        P("group", None, ("shard", "tensor")),
        P("group", ("shard", "tensor")),
        P("tensor", "shard"),
        P("group", "tensor", "shard"),
        P("tensor", "shard"),
        P(None, "shard"),
    )
    return jax.shard_map(
        body,
        mesh=mesh,
        in_specs=placed,
        out_specs=(
            P("shard", "tensor"),
            P(("shard", "group"), "tensor"),
            P(None, ("shard", "tensor")),
            P("group", ("shard", "tensor")),
            P("tensor", "shard"),
            P("tensor", "shard"),
        ),
        check_vma=False,
    )
```

```python
import jax
import jax.numpy as jnp
from jax import lax
from jax.experimental import pallas as pl
from jax.experimental.pallas import tpu as pltpu
from jax.sharding import PartitionSpec as P

outer_rate = 0.7
momentum = 0.9
groups = 2

local_weight = outer_rate * (1.0 + momentum) / groups
moment_weight = outer_rate * momentum * momentum
anchor_weight = 1.0 - outer_rate * (1.0 + momentum)

SIDE = 4
HIGHEST = lax.Precision.HIGHEST
MESH = pl.DeviceIdType.MESH


def ring(s, axis_x):
    x, y, core = s // (2 * SIDE), (s // 2) % SIDE, s % 2

    def along_x(d):
        return {"shard": ((x + d) % SIDE) * 2 * SIDE + y * 2 + core}

    def along_y(d):
        return {"shard": x * 2 * SIDE + ((y + d) % SIDE) * 2 + core}

    return along_x if axis_x else along_y


def remote(src, dst, send, recv, device):
    return pltpu.make_async_remote_copy(
        src_ref=src, dst_ref=dst, send_sem=send, recv_sem=recv, device_id=device, device_id_type=MESH
    )


def meet(partners):
    barrier = pltpu.get_barrier_semaphore()
    for device in partners:
        pl.semaphore_signal(barrier, inc=1, device_id=device, device_id_type=MESH)
    pl.semaphore_wait(barrier, len(partners))


def take_raw(down_local, raw, sem):
    half = raw.shape[0]
    g = lax.axis_index("group")
    theirs = pl.ds(pl.multiple_of((1 - g) * half, half), half)
    copy = pltpu.make_async_copy(down_local.at[0, theirs], raw, sem)
    copy.start()
    copy.wait()


def combine(down_local, down_moment, raw, part, dl, dm, sem):
    half = part.shape[0]
    g = lax.axis_index("group")
    mine = pl.ds(pl.multiple_of(g * half, half), half)
    loads = [
        pltpu.make_async_copy(down_local.at[0, mine], dl, sem.at[0]),
        pltpu.make_async_copy(down_moment, dm, sem.at[1]),
    ]
    for load in loads:
        load.start()
    for load in loads:
        load.wait()

    def block(i, carry):
        rows = pl.ds(pl.multiple_of(i * 16, 16), 16)
        part[rows, :] = local_weight * dl[rows, :] - moment_weight * dm[rows, :]
        return carry

    lax.fori_loop(0, half // 16, block, 0)


def reduce_factors(
    gate_anchor, gate_local, factor_basis, norm_local, norm_moment, out,
    ga, gl, basis, away, home, from_core, from_x, row, from_y,
    load_sem, core_send, core_recv, x_send, x_recv, y_send, y_recv,
):
    s = lax.axis_index("shard")
    x, y, core = s // (2 * SIDE), (s // 2) % SIDE, s % 2
    along_x, along_y = ring(s, True), ring(s, False)
    other_core = {"shard": s + 1 - 2 * core}
    wide = gl.shape[0] // 2
    span = wide // SIDE
    tall = from_y.shape[1]
    near = pl.ds(pl.multiple_of(core * wide, wide), wide)
    far = pl.ds(pl.multiple_of((1 - core) * wide, wide), wide)
    pairs = [
        (factor_basis, basis),
        (gate_anchor.at[far], ga.at[far]),
        (gate_local.at[0, far], gl.at[far]),
        (gate_anchor.at[near], ga.at[near]),
        (gate_local.at[0, near], gl.at[near]),
    ]
    loads = [pltpu.make_async_copy(src, dst, load_sem.at[i]) for i, (src, dst) in enumerate(pairs)]
    for load in loads:
        load.start()
    meet([other_core] + [along_x(d) for d in range(1, SIDE)] + [along_y(d) for d in range(1, SIDE)])

    def factor(start, target):
        def block(i, carry):
            rows = pl.ds(pl.multiple_of(start + i * span, span), span)
            diff = ga[rows, :] - gl[rows, :]
            target[i] = lax.dot_general(
                basis[...], diff, (((1,), (1,)), ((), ())), precision=HIGHEST, preferred_element_type=jnp.float32
            )
            return carry

        lax.fori_loop(0, SIDE, block, 0)

    for load in loads[:3]:
        load.wait()
    factor((1 - core) * wide, away)
    core_copy = remote(away, from_core, core_send, core_recv, other_core)
    core_copy.start()
    for load in loads[3:5]:
        load.wait()
    factor(core * wide, home)
    out[tall:, :] = jnp.zeros((8, span), jnp.float32)
    out[tall : tall + 2, 0 : norm_local.shape[2]] = norm_local[0]
    out[tall + 2 : tall + 3, 0 : norm_local.shape[2]] = norm_moment[...]
    core_copy.wait_recv()
    x_copies = []
    for d in (2, 1, 3):
        to = (x + d) % SIDE
        home[to] = home[to] + from_core[to]
        x_copies.append(remote(home.at[to], from_x.at[d - 1], x_send.at[d - 1], x_recv.at[d - 1], along_x(d)))
        x_copies[-1].start()
    row[...] = home[x] + from_core[x]
    for copy in x_copies:
        copy.wait_recv()
    row[...] = (row[...] + from_x[0]) + (from_x[1] + from_x[2])
    y_copies = []
    for d in (2, 1, 3):
        rows = pl.ds(pl.multiple_of(((y + d) % SIDE) * tall, tall), tall)
        y_copies.append(remote(row.at[rows], from_y.at[d - 1], y_send.at[d - 1], y_recv.at[d - 1], along_y(d)))
        y_copies[-1].start()
    kept = pl.ds(pl.multiple_of(y * tall, tall), tall)
    for copy in y_copies:
        copy.wait_recv()
    out[0:tall, :] = (row[kept, :] + from_y[0]) + (from_y[1] + from_y[2])
    for copy in [core_copy] + x_copies + y_copies:
        copy.wait_send()


def gather_factors(
    own, peer, norm_anchor, out, new_norm_anchor, new_norm_moment,
    whole, core_send, core_recv, x_send, x_recv, y_send, y_recv,
):
    g = lax.axis_index("group")
    s = lax.axis_index("shard")
    x, y, core = s // (2 * SIDE), (s // 2) % SIDE, s % 2
    along_x, along_y = ring(s, True), ring(s, False)
    other_core = {"shard": s + 1 - 2 * core}
    tall = whole.shape[1] // SIDE
    meet([other_core] + [along_x(d) for d in range(1, SIDE)] + [along_y(d) for d in range(1, SIDE)])
    slot = core * SIDE + x
    kept = pl.ds(pl.multiple_of(y * tall, tall), tall)
    whole[slot, kept, :] = (own[0:tall, :] + peer[0:tall, :]) * (1.0 / groups)
    y_back = []
    for d in (2, 1, 3):
        here = whole.at[slot, kept]
        y_back.append(remote(here, here, y_send.at[d - 1], y_recv.at[d - 1], along_y(d)))
        y_back[-1].start()
    lanes = norm_anchor.shape[1]
    ours = own[tall : tall + 8, 0:lanes]
    theirs = peer[tall : tall + 8, 0:lanes]
    norm_delta = norm_anchor[...] - (ours[0:2] + theirs[0:2]) * (1.0 / groups)
    picked = lax.broadcasted_iota(jnp.int32, norm_anchor.shape, 0) == g
    norm_next = momentum * jnp.where(picked, ours[2:3], theirs[2:3]) + norm_delta
    new_norm_anchor[...] = norm_anchor[...] - outer_rate * (norm_delta + momentum * norm_next)
    new_norm_moment[...] = jnp.where(g == 0, norm_next[0:1], norm_next[1:2])
    for copy in y_back:
        copy.wait_recv()
    x_back = []
    for d in (2, 1, 3):
        here = whole.at[slot]
        x_back.append(remote(here, here, x_send.at[d - 1], x_recv.at[d - 1], along_x(d)))
        x_back[-1].start()
    for copy in x_back:
        copy.wait_recv()
    half = whole.at[pl.ds(pl.multiple_of(core * SIDE, SIDE), SIDE)]
    core_back = remote(half, half, core_send, core_recv, other_core)
    core_back.start()
    core_back.wait_recv()

    def move(i, carry):
        out[i] = whole[i]
        return carry

    lax.fori_loop(0, 2 * SIDE, move, 0)
    for copy in y_back + x_back + [core_back]:
        copy.wait_send()


def rebuild(
    gate_anchor, gate_moment, factor_basis, whole, norm_a, norm_m,
    new_anchor, new_moment, new_norm_anchor, new_norm_moment, ga, gm, load_sem, store_sem,
):
    blocks = whole.shape[0]
    span = whole.shape[2]
    loads, stores = [], []
    for i in range(blocks):
        rows = pl.ds(i * span, span)
        loads.append(pltpu.make_async_copy(gate_anchor.at[rows], ga.at[rows], load_sem.at[2 * i]))
        loads.append(pltpu.make_async_copy(gate_moment.at[rows], gm.at[rows], load_sem.at[2 * i + 1]))
        stores.append(pltpu.make_async_copy(ga.at[rows], new_anchor.at[rows], store_sem.at[2 * i]))
        stores.append(pltpu.make_async_copy(gm.at[rows], new_moment.at[rows], store_sem.at[2 * i + 1]))
    for load in loads:
        load.start()
    new_norm_anchor[...] = norm_a[...]
    new_norm_moment[...] = norm_m[...]
    for i in range(blocks):
        rows = pl.ds(i * span, span)
        delta = lax.dot_general(
            whole[i], factor_basis[...], (((0,), (0,)), ((), ())), precision=HIGHEST,
            preferred_element_type=jnp.float32,
        )
        loads[2 * i].wait()
        loads[2 * i + 1].wait()
        moment = momentum * gm[rows, :] + delta
        gm[rows, :] = moment
        ga[rows, :] = ga[rows, :] - outer_rate * (delta + momentum * moment)
        stores[2 * i].start()
        stores[2 * i + 1].start()
    for store in stores:
        store.wait()


def own_half(
    down_anchor, down_moment, raw, peer, down_local, part,
    new_anchor, new_moment, base, da, dm, dl, pr, load_sem, store_sem,
):
    half = part.shape[0]
    g = lax.axis_index("group")
    mine = pl.ds(pl.multiple_of(g * half, half), half)
    pairs = [
        (down_anchor, da),
        (down_moment, dm),
        (down_local.at[0, mine], dl),
        (peer, pr),
    ]
    loads = [pltpu.make_async_copy(src, dst, load_sem.at[i]) for i, (src, dst) in enumerate(pairs)]
    for load in loads:
        load.start()
    for load in loads:
        load.wait()

    def block(i, carry):
        rows = pl.ds(pl.multiple_of(i * 16, 16), 16)
        own = pl.ds(pl.multiple_of(g * half + i * 16, 16), 16)
        anchor = da[own, :]
        dm[rows, :] = momentum * dm[rows, :] + (anchor - (dl[rows, :] + pr[rows, :]) * (1.0 / groups))
        da[own, :] = (anchor_weight * anchor + local_weight * pr[rows, :]) + part[rows, :]
        far = pl.ds(pl.multiple_of((1 - g) * half + i * 16, 16), 16)
        base[rows, :] = anchor_weight * da[far, :] + local_weight * raw[rows, :]
        return carry

    lax.fori_loop(0, half // 16, block, 0)
    stores = [
        pltpu.make_async_copy(da.at[mine], new_anchor.at[mine], store_sem.at[0]),
        pltpu.make_async_copy(dm, new_moment, store_sem.at[1]),
    ]
    for store in stores:
        store.start()
    for store in stores:
        store.wait()


def other_half(given, base, peer, new_anchor, result, sem):
    del given
    half = base.shape[0]
    chunks = sem.shape[0]
    step = half // chunks
    g = lax.axis_index("group")
    stores = []
    for c in range(chunks):
        def block(i, carry):
            rows = pl.ds(pl.multiple_of(c * step + i * 8, 8), 8)
            result[rows, :] = base[rows, :] + peer[rows, :]
            return carry

        lax.fori_loop(0, step // 8, block, 0)
        rows = pl.ds(c * step, step)
        far = pl.ds(pl.multiple_of((1 - g) * half + c * step, step), step)
        stores.append(pltpu.make_async_copy(result.at[rows], new_anchor.at[far], sem.at[c]))
        stores[-1].start()
    for store in stores:
        store.wait()


def body(*args):
    (down_anchor, down_local, down_moment, norm_anchor, norm_local, norm_moment, gate_anchor, gate_local, gate_moment,
     factor_basis) = args
    f32 = jnp.float32
    half, width = down_moment.shape
    rank, depth = factor_basis.shape
    hidden = gate_anchor.shape[0]
    wide = hidden // 2
    span = wide // SIDE
    tall = rank // SIDE
    anywhere = pl.BlockSpec(memory_space=pl.ANY)
    vmem = pl.BlockSpec(memory_space=pltpu.VMEM)
    dma = pltpu.SemaphoreType.DMA
    V = lambda *shape: pltpu.VMEM(shape, f32)
    S = lambda a: jax.ShapeDtypeStruct(a.shape, f32)
    swap = [(0, 1), (1, 0)]

    def cost(us):
        return pl.CostEstimate(flops=0, bytes_accessed=int(us * 3.5e6), transcendentals=0)

    def params(mib, **more):
        return pltpu.CompilerParams(vmem_limit_bytes=mib << 20, **more)

    raw = pl.pallas_call(
        take_raw, out_shape=V(half, width), in_specs=[pl.BlockSpec(memory_space=pltpu.HBM)], out_specs=vmem, scratch_shapes=[dma],
        compiler_params=params(8), cost_estimate=cost(1),
    )(down_local)
    peer_raw = lax.ppermute(raw, "group", swap)
    part = pl.pallas_call(
        combine, out_shape=V(half, width), in_specs=[anywhere] * 2 + [vmem], out_specs=vmem,
        scratch_shapes=[V(half, width), V(half, width), dma((2,))], compiler_params=params(8), cost_estimate=cost(2),
    )(down_local, down_moment, raw)
    own = pl.pallas_call(
        reduce_factors,
        out_shape=V(tall + 8, span),
        in_specs=[anywhere] * 2 + [vmem] * 3,
        out_specs=vmem,
        scratch_shapes=[
            V(hidden, depth), V(hidden, depth), V(rank, depth), V(SIDE, rank, span), V(SIDE, rank, span),
            V(SIDE, rank, span), V(SIDE - 1, rank, span), V(rank, span), V(SIDE - 1, tall, span),
            dma((5,)), dma, dma, dma((3,)), dma((3,)), dma((3,)), dma((3,)),
        ],
        compiler_params=params(16, collective_id=0, has_side_effects=True), cost_estimate=cost(20),
    )(gate_anchor, gate_local, factor_basis, norm_local, norm_moment)
    peer = lax.ppermute(own, "group", swap)
    peer, part = lax.optimization_barrier((peer, part))
    peer_part = lax.ppermute(part, "group", swap)
    whole, norm_a, norm_m = pl.pallas_call(
        gather_factors,
        out_shape=[V(2 * SIDE, rank, span), V(*norm_anchor.shape), V(*norm_moment.shape)],
        in_specs=[vmem] * 3,
        out_specs=[vmem] * 3,
        scratch_shapes=[V(2 * SIDE, rank, span), dma, dma, dma((3,)), dma((3,)), dma((3,)), dma((3,))],
        compiler_params=params(8, collective_id=1, has_side_effects=True), cost_estimate=cost(15),
    )(own, peer, norm_anchor)
    new_gate_anchor, new_gate_moment, new_norm_anchor, new_norm_moment = pl.pallas_call(
        rebuild,
        out_shape=[S(gate_anchor), S(gate_moment), S(norm_anchor), S(norm_moment)],
        in_specs=[anywhere] * 2 + [vmem] * 4,
        out_specs=[anywhere] * 2 + [vmem] * 2,
        scratch_shapes=[V(hidden, depth), V(hidden, depth), dma((4 * SIDE,)), dma((4 * SIDE,))],
        compiler_params=params(16), cost_estimate=cost(5),
    )(gate_anchor, gate_moment, factor_basis, whole, norm_a, norm_m)
    peer_raw, _ = lax.optimization_barrier((peer_raw, whole))
    anchor, new_down_moment, base = pl.pallas_call(
        own_half,
        out_shape=[S(down_anchor), S(down_moment), V(half, width)],
        in_specs=[anywhere] * 2 + [vmem, anywhere, anywhere, vmem],
        out_specs=[anywhere] * 2 + [vmem],
        scratch_shapes=[V(2 * half, width)] + [V(half, width)] * 3 + [dma((4,)), dma((2,))],
        compiler_params=params(16), cost_estimate=cost(4),
    )(down_anchor, down_moment, raw, peer_raw, down_local, part)
    new_down_anchor = pl.pallas_call(
        other_half,
        out_shape=S(down_anchor),
        in_specs=[anywhere, vmem, vmem],
        out_specs=anywhere,
        input_output_aliases={0: 0},
        scratch_shapes=[V(half, width), dma((4,))],
        compiler_params=params(8), cost_estimate=cost(1),
    )(anchor, base, peer_part)
    return new_down_anchor, new_down_moment, new_norm_anchor, new_norm_moment, new_gate_anchor, new_gate_moment


def solution(mesh):
    placed = (
        P("shard", "tensor"),
        P("group", "shard", "tensor"),
        P(("shard", "group"), "tensor"),
        P(None, ("shard", "tensor")),
        P("group", None, ("shard", "tensor")),
        P("group", ("shard", "tensor")),
        P("tensor", "shard"),
        P("group", "tensor", "shard"),
        P("tensor", "shard"),
        P(None, "shard"),
    )
    return jax.shard_map(
        body,
        mesh=mesh,
        in_specs=placed,
        out_specs=(
            P("shard", "tensor"),
            P(("shard", "group"), "tensor"),
            P(None, ("shard", "tensor")),
            P("group", ("shard", "tensor")),
            P("tensor", "shard"),
            P("tensor", "shard"),
        ),
        check_vma=False,
    )
```

```python
import jax
import jax.numpy as jnp
from jax import lax
from jax.experimental import pallas as pl
from jax.experimental.pallas import tpu as pltpu
from jax.sharding import PartitionSpec as P

outer_rate = 0.7
momentum = 0.9
groups = 2

local_weight = outer_rate * (1.0 + momentum) / groups
moment_weight = outer_rate * momentum * momentum
anchor_weight = 1.0 - outer_rate * (1.0 + momentum)

SIDE = 4
HIGHEST = lax.Precision.HIGHEST
MESH = pl.DeviceIdType.MESH


def ring(s, axis_x):
    x, y, core = s // (2 * SIDE), (s // 2) % SIDE, s % 2

    def along_x(d):
        return {"shard": ((x + d) % SIDE) * 2 * SIDE + y * 2 + core}

    def along_y(d):
        return {"shard": x * 2 * SIDE + ((y + d) % SIDE) * 2 + core}

    return along_x if axis_x else along_y


def remote(src, dst, send, recv, device):
    return pltpu.make_async_remote_copy(
        src_ref=src, dst_ref=dst, send_sem=send, recv_sem=recv, device_id=device, device_id_type=MESH
    )


def meet(partners):
    barrier = pltpu.get_barrier_semaphore()
    for device in partners:
        pl.semaphore_signal(barrier, inc=1, device_id=device, device_id_type=MESH)
    pl.semaphore_wait(barrier, len(partners))


def take_raw(down_local, raw, sem):
    half = raw.shape[0]
    g = lax.axis_index("group")
    theirs = pl.ds(pl.multiple_of((1 - g) * half, half), half)
    copy = pltpu.make_async_copy(down_local.at[0, theirs], raw, sem)
    copy.start()
    copy.wait()


def combine(down_local, down_moment, raw, part, dl, dm, sem):
    half = part.shape[0]
    g = lax.axis_index("group")
    mine = pl.ds(pl.multiple_of(g * half, half), half)
    loads = [
        pltpu.make_async_copy(down_local.at[0, mine], dl, sem.at[0]),
        pltpu.make_async_copy(down_moment, dm, sem.at[1]),
    ]
    for load in loads:
        load.start()
    for load in loads:
        load.wait()

    def block(i, carry):
        rows = pl.ds(pl.multiple_of(i * 16, 16), 16)
        part[rows, :] = local_weight * dl[rows, :] - moment_weight * dm[rows, :]
        return carry

    lax.fori_loop(0, half // 16, block, 0)


def reduce_factors(
    gate_anchor, gate_local, factor_basis, norm_local, norm_moment, out,
    ga, gl, basis, away, home, from_core, from_x, via, row, from_y,
    load_sem, core_send, core_recv, x_send, x_recv, y_send, y_recv,
):
    s = lax.axis_index("shard")
    x, y, core = s // (2 * SIDE), (s // 2) % SIDE, s % 2
    along_x, along_y = ring(s, True), ring(s, False)
    other_core = {"shard": s + 1 - 2 * core}
    wide = gl.shape[0] // 2
    span = wide // SIDE
    tall = from_y.shape[1]
    near = pl.ds(pl.multiple_of(core * wide, wide), wide)
    far = pl.ds(pl.multiple_of((1 - core) * wide, wide), wide)
    pairs = [
        (factor_basis, basis),
        (gate_anchor.at[far], ga.at[far]),
        (gate_local.at[0, far], gl.at[far]),
        (gate_anchor.at[near], ga.at[near]),
        (gate_local.at[0, near], gl.at[near]),
    ]
    loads = [pltpu.make_async_copy(src, dst, load_sem.at[i]) for i, (src, dst) in enumerate(pairs)]
    for load in loads:
        load.start()
    meet([other_core, along_x(1), along_x(3)] + [along_y(d) for d in range(1, SIDE)])

    def factor(start, target):
        def block(i, carry):
            rows = pl.ds(pl.multiple_of(start + i * span, span), span)
            diff = ga[rows, :] - gl[rows, :]
            target[i] = lax.dot_general(
                basis[...], diff, (((1,), (1,)), ((), ())), precision=HIGHEST, preferred_element_type=jnp.float32
            )
            return carry

        lax.fori_loop(0, SIDE, block, 0)

    for load in loads[:3]:
        load.wait()
    factor((1 - core) * wide, away)
    core_copy = remote(away, from_core, core_send, core_recv, other_core)
    core_copy.start()
    for load in loads[3:5]:
        load.wait()
    factor(core * wide, home)
    out[tall:, :] = jnp.zeros((8, span), jnp.float32)
    out[tall : tall + 2, 0 : norm_local.shape[2]] = norm_local[0]
    out[tall + 2 : tall + 3, 0 : norm_local.shape[2]] = norm_moment[...]
    core_copy.wait_recv()
    rank = row.shape[0]
    top, low = pl.ds(0, rank // 2), pl.ds(rank // 2, rank // 2)
    up, across, down = (x + 1) % SIDE, (x + 2) % SIDE, (x + 3) % SIDE

    def send_x(i, src, dst, d):
        copy = remote(src, dst, x_send.at[i], x_recv.at[i], along_x(d))
        copy.start()
        return copy

    home[across] = home[across] + from_core[across]
    x_copies = [
        send_x(0, home.at[across, top], via.at[0], 1),
        send_x(1, home.at[across, low], via.at[1], 3),
    ]
    home[up] = home[up] + from_core[up]
    x_copies.append(send_x(2, home.at[up, low], from_x.at[0, low], 1))
    home[down] = home[down] + from_core[down]
    x_copies.append(send_x(3, home.at[down, top], from_x.at[1, top], 3))
    row[...] = home[x] + from_core[x]
    x_copies[0].wait_recv()
    home[up, top, :] = home[up, top, :] + via[0]
    x_copies.append(send_x(4, home.at[up, top], from_x.at[0, top], 1))
    x_copies[1].wait_recv()
    home[down, low, :] = home[down, low, :] + via[1]
    x_copies.append(send_x(5, home.at[down, low], from_x.at[1, low], 3))
    for copy in x_copies[2:]:
        copy.wait_recv()
    row[...] = row[...] + (from_x[0] + from_x[1])
    y_copies = []
    for d in (2, 1, 3):
        rows = pl.ds(pl.multiple_of(((y + d) % SIDE) * tall, tall), tall)
        y_copies.append(remote(row.at[rows], from_y.at[d - 1], y_send.at[d - 1], y_recv.at[d - 1], along_y(d)))
        y_copies[-1].start()
    kept = pl.ds(pl.multiple_of(y * tall, tall), tall)
    for copy in y_copies:
        copy.wait_recv()
    out[0:tall, :] = (row[kept, :] + from_y[0]) + (from_y[1] + from_y[2])
    for copy in [core_copy] + x_copies + y_copies:
        copy.wait_send()


def gather_factors(
    own, peer, norm_anchor, out, new_norm_anchor, new_norm_moment,
    whole, core_send, core_recv, x_send, x_recv, y_send, y_recv,
):
    g = lax.axis_index("group")
    s = lax.axis_index("shard")
    x, y, core = s // (2 * SIDE), (s // 2) % SIDE, s % 2
    along_x, along_y = ring(s, True), ring(s, False)
    other_core = {"shard": s + 1 - 2 * core}
    tall = whole.shape[1] // SIDE
    meet([other_core] + [along_x(d) for d in range(1, SIDE)] + [along_y(d) for d in range(1, SIDE)])
    slot = core * SIDE + x
    kept = pl.ds(pl.multiple_of(y * tall, tall), tall)
    whole[slot, kept, :] = (own[0:tall, :] + peer[0:tall, :]) * (1.0 / groups)
    y_back = []
    for d in (2, 1, 3):
        here = whole.at[slot, kept]
        y_back.append(remote(here, here, y_send.at[d - 1], y_recv.at[d - 1], along_y(d)))
        y_back[-1].start()
    lanes = norm_anchor.shape[1]
    ours = own[tall : tall + 8, 0:lanes]
    theirs = peer[tall : tall + 8, 0:lanes]
    norm_delta = norm_anchor[...] - (ours[0:2] + theirs[0:2]) * (1.0 / groups)
    picked = lax.broadcasted_iota(jnp.int32, norm_anchor.shape, 0) == g
    norm_next = momentum * jnp.where(picked, ours[2:3], theirs[2:3]) + norm_delta
    new_norm_anchor[...] = norm_anchor[...] - outer_rate * (norm_delta + momentum * norm_next)
    new_norm_moment[...] = jnp.where(g == 0, norm_next[0:1], norm_next[1:2])
    for copy in y_back:
        copy.wait_recv()
    x_back = []
    for d in (2, 1, 3):
        here = whole.at[slot]
        x_back.append(remote(here, here, x_send.at[d - 1], x_recv.at[d - 1], along_x(d)))
        x_back[-1].start()
    for copy in x_back:
        copy.wait_recv()
    half = whole.at[pl.ds(pl.multiple_of(core * SIDE, SIDE), SIDE)]
    core_back = remote(half, half, core_send, core_recv, other_core)
    core_back.start()
    core_back.wait_recv()

    def move(i, carry):
        out[i] = whole[i]
        return carry

    lax.fori_loop(0, 2 * SIDE, move, 0)
    for copy in y_back + x_back + [core_back]:
        copy.wait_send()


def rebuild(
    gate_anchor, gate_moment, factor_basis, whole, norm_a, norm_m,
    new_anchor, new_moment, new_norm_anchor, new_norm_moment, ga, gm, store_sem,
):
    blocks = whole.shape[0]
    span = whole.shape[2]
    stores = []
    for i in range(blocks):
        rows = pl.ds(i * span, span)
        stores.append(pltpu.make_async_copy(ga.at[rows], new_anchor.at[rows], store_sem.at[2 * i]))
        stores.append(pltpu.make_async_copy(gm.at[rows], new_moment.at[rows], store_sem.at[2 * i + 1]))
    new_norm_anchor[...] = norm_a[...]
    new_norm_moment[...] = norm_m[...]
    for i in range(blocks):
        rows = pl.ds(i * span, span)
        delta = lax.dot_general(
            whole[i], factor_basis[...], (((0,), (0,)), ((), ())), precision=HIGHEST,
            preferred_element_type=jnp.float32,
        )
        moment = momentum * gate_moment[rows, :] + delta
        gm[rows, :] = moment
        ga[rows, :] = gate_anchor[rows, :] - outer_rate * (delta + momentum * moment)
        stores[2 * i].start()
        stores[2 * i + 1].start()
    for store in stores:
        store.wait()


def own_half(
    down_anchor, down_moment, raw, peer, down_local, part,
    new_anchor, new_moment, base, da, dm, dl, pr, load_sem, store_sem,
):
    half = part.shape[0]
    g = lax.axis_index("group")
    mine = pl.ds(pl.multiple_of(g * half, half), half)
    pairs = [
        (down_anchor, da),
        (down_moment, dm),
        (down_local.at[0, mine], dl),
        (peer, pr),
    ]
    loads = [pltpu.make_async_copy(src, dst, load_sem.at[i]) for i, (src, dst) in enumerate(pairs)]
    for load in loads:
        load.start()
    for load in loads:
        load.wait()

    def block(i, carry):
        rows = pl.ds(pl.multiple_of(i * 16, 16), 16)
        own = pl.ds(pl.multiple_of(g * half + i * 16, 16), 16)
        anchor = da[own, :]
        dm[rows, :] = momentum * dm[rows, :] + (anchor - (dl[rows, :] + pr[rows, :]) * (1.0 / groups))
        da[own, :] = (anchor_weight * anchor + local_weight * pr[rows, :]) + part[rows, :]
        far = pl.ds(pl.multiple_of((1 - g) * half + i * 16, 16), 16)
        base[rows, :] = anchor_weight * da[far, :] + local_weight * raw[rows, :]
        return carry

    lax.fori_loop(0, half // 16, block, 0)
    stores = [
        pltpu.make_async_copy(da.at[mine], new_anchor.at[mine], store_sem.at[0]),
        pltpu.make_async_copy(dm, new_moment, store_sem.at[1]),
    ]
    for store in stores:
        store.start()
    for store in stores:
        store.wait()


def other_half(given, base, peer, new_anchor, result, sem):
    del given
    half = base.shape[0]
    chunks = sem.shape[0]
    step = half // chunks
    g = lax.axis_index("group")
    stores = []
    for c in range(chunks):
        def block(i, carry):
            rows = pl.ds(pl.multiple_of(c * step + i * 8, 8), 8)
            result[rows, :] = base[rows, :] + peer[rows, :]
            return carry

        lax.fori_loop(0, step // 8, block, 0)
        rows = pl.ds(c * step, step)
        far = pl.ds(pl.multiple_of((1 - g) * half + c * step, step), step)
        stores.append(pltpu.make_async_copy(result.at[rows], new_anchor.at[far], sem.at[c]))
        stores[-1].start()
    for store in stores:
        store.wait()


def body(*args):
    (down_anchor, down_local, down_moment, norm_anchor, norm_local, norm_moment, gate_anchor, gate_local, gate_moment,
     factor_basis) = args
    f32 = jnp.float32
    half, width = down_moment.shape
    rank, depth = factor_basis.shape
    hidden = gate_anchor.shape[0]
    wide = hidden // 2
    span = wide // SIDE
    tall = rank // SIDE
    anywhere = pl.BlockSpec(memory_space=pl.ANY)
    vmem = pl.BlockSpec(memory_space=pltpu.VMEM)
    dma = pltpu.SemaphoreType.DMA
    V = lambda *shape: pltpu.VMEM(shape, f32)
    S = lambda a: jax.ShapeDtypeStruct(a.shape, f32)
    swap = [(0, 1), (1, 0)]

    def cost(us):
        return pl.CostEstimate(flops=0, bytes_accessed=int(us * 3.5e6), transcendentals=0)

    def params(mib, **more):
        return pltpu.CompilerParams(vmem_limit_bytes=mib << 20, **more)

    raw = pl.pallas_call(
        take_raw, out_shape=V(half, width), in_specs=[pl.BlockSpec(memory_space=pltpu.HBM)], out_specs=vmem, scratch_shapes=[dma],
        compiler_params=params(60), cost_estimate=cost(1),
    )(down_local)
    peer_raw = lax.ppermute(raw, "group", swap)
    part = pl.pallas_call(
        combine, out_shape=V(half, width), in_specs=[anywhere] * 2 + [vmem], out_specs=vmem,
        scratch_shapes=[V(half, width), V(half, width), dma((2,))], compiler_params=params(8), cost_estimate=cost(2),
    )(down_local, down_moment, raw)
    own = pl.pallas_call(
        reduce_factors,
        out_shape=V(tall + 8, span),
        in_specs=[anywhere] * 2 + [vmem] * 3,
        out_specs=vmem,
        scratch_shapes=[
            V(hidden, depth), V(hidden, depth), V(rank, depth), V(SIDE, rank, span), V(SIDE, rank, span),
            V(SIDE, rank, span), V(2, rank, span), V(2, rank // 2, span), V(rank, span), V(SIDE - 1, tall, span),
            dma((5,)), dma, dma, dma((6,)), dma((6,)), dma((3,)), dma((3,)),
        ],
        compiler_params=params(16, collective_id=0, has_side_effects=True), cost_estimate=cost(20),
    )(gate_anchor, gate_local, factor_basis, norm_local, norm_moment)
    peer = lax.ppermute(own, "group", swap)
    peer_raw, _ = lax.optimization_barrier((peer_raw, own))
    anchor, new_down_moment, base = pl.pallas_call(
        own_half,
        out_shape=[S(down_anchor), S(down_moment), V(half, width)],
        in_specs=[anywhere] * 2 + [vmem, anywhere, anywhere, vmem],
        out_specs=[anywhere] * 2 + [vmem],
        scratch_shapes=[V(2 * half, width)] + [V(half, width)] * 3 + [dma((4,)), dma((2,))],
        compiler_params=params(16), cost_estimate=cost(4),
    )(down_anchor, down_moment, raw, peer_raw, down_local, part)
    peer, base, part = lax.optimization_barrier((peer, base, part))
    peer_part = lax.ppermute(part, "group", swap)
    whole, norm_a, norm_m = pl.pallas_call(
        gather_factors,
        out_shape=[V(2 * SIDE, rank, span), V(*norm_anchor.shape), V(*norm_moment.shape)],
        in_specs=[vmem] * 3,
        out_specs=[vmem] * 3,
        scratch_shapes=[V(2 * SIDE, rank, span), dma, dma, dma((3,)), dma((3,)), dma((3,)), dma((3,))],
        compiler_params=params(8, collective_id=1, has_side_effects=True), cost_estimate=cost(15),
    )(own, peer, norm_anchor)
    new_gate_anchor, new_gate_moment, new_norm_anchor, new_norm_moment = pl.pallas_call(
        rebuild,
        out_shape=[S(gate_anchor), S(gate_moment), S(norm_anchor), S(norm_moment)],
        in_specs=[vmem] * 6,
        out_specs=[anywhere] * 2 + [vmem] * 2,
        scratch_shapes=[V(hidden, depth), V(hidden, depth), dma((4 * SIDE,))],
        compiler_params=params(16), cost_estimate=cost(5),
    )(gate_anchor, gate_moment, factor_basis, whole, norm_a, norm_m)
    new_down_anchor = pl.pallas_call(
        other_half,
        out_shape=S(down_anchor),
        in_specs=[anywhere, vmem, vmem],
        out_specs=anywhere,
        input_output_aliases={0: 0},
        scratch_shapes=[V(half, width), dma((4,))],
        compiler_params=params(8), cost_estimate=cost(1),
    )(anchor, base, peer_part)
    return new_down_anchor, new_down_moment, new_norm_anchor, new_norm_moment, new_gate_anchor, new_gate_moment


def solution(mesh):
    placed = (
        P("shard", "tensor"),
        P("group", "shard", "tensor"),
        P(("shard", "group"), "tensor"),
        P(None, ("shard", "tensor")),
        P("group", None, ("shard", "tensor")),
        P("group", ("shard", "tensor")),
        P("tensor", "shard"),
        P("group", "tensor", "shard"),
        P("tensor", "shard"),
        P(None, "shard"),
    )
    return jax.shard_map(
        body,
        mesh=mesh,
        in_specs=placed,
        out_specs=(
            P("shard", "tensor"),
            P(("shard", "group"), "tensor"),
            P(None, ("shard", "tensor")),
            P("group", ("shard", "tensor")),
            P("tensor", "shard"),
            P("tensor", "shard"),
        ),
        check_vma=False,
    )
```

```python
import jax
import jax.numpy as jnp
from jax import lax
from jax.experimental import pallas as pl
from jax.experimental.pallas import tpu as pltpu
from jax.sharding import PartitionSpec as P

outer_rate = 0.7
momentum = 0.9
groups = 2

local_weight = outer_rate * (1.0 + momentum) / groups
moment_weight = outer_rate * momentum * momentum
anchor_weight = 1.0 - outer_rate * (1.0 + momentum)

SIDE = 4
HIGHEST = lax.Precision.HIGHEST
MESH = pl.DeviceIdType.MESH


def ring(s, axis_x):
    x, y, core = s // (2 * SIDE), (s // 2) % SIDE, s % 2

    def along_x(d):
        return {"shard": ((x + d) % SIDE) * 2 * SIDE + y * 2 + core}

    def along_y(d):
        return {"shard": x * 2 * SIDE + ((y + d) % SIDE) * 2 + core}

    return along_x if axis_x else along_y


def remote(src, dst, send, recv, device):
    return pltpu.make_async_remote_copy(
        src_ref=src, dst_ref=dst, send_sem=send, recv_sem=recv, device_id=device, device_id_type=MESH
    )


def meet(partners):
    barrier = pltpu.get_barrier_semaphore()
    for device in partners:
        pl.semaphore_signal(barrier, inc=1, device_id=device, device_id_type=MESH)
    pl.semaphore_wait(barrier, len(partners))


def take_raw(down_local, raw, sem):
    half = raw.shape[0]
    g = lax.axis_index("group")
    theirs = pl.ds(pl.multiple_of((1 - g) * half, half), half)
    copy = pltpu.make_async_copy(down_local.at[0, theirs], raw, sem)
    copy.start()
    copy.wait()


def combine(down_local, down_moment, raw, part, dl, dm, sem):
    half = part.shape[0]
    g = lax.axis_index("group")
    mine = pl.ds(pl.multiple_of(g * half, half), half)
    loads = [
        pltpu.make_async_copy(down_local.at[0, mine], dl, sem.at[0]),
        pltpu.make_async_copy(down_moment, dm, sem.at[1]),
    ]
    for load in loads:
        load.start()
    for load in loads:
        load.wait()

    def block(i, carry):
        rows = pl.ds(pl.multiple_of(i * 16, 16), 16)
        part[rows, :] = local_weight * dl[rows, :] - moment_weight * dm[rows, :]
        return carry

    lax.fori_loop(0, half // 16, block, 0)


def reduce_factors(
    gate_anchor, gate_local, factor_basis, norm_local, norm_moment, out,
    ga, gl, basis, away, home, from_core, from_x, via, row, from_y,
    load_sem, core_send, core_recv, x_send, x_recv, y_send, y_recv,
):
    s = lax.axis_index("shard")
    x, y, core = s // (2 * SIDE), (s // 2) % SIDE, s % 2
    along_x, along_y = ring(s, True), ring(s, False)
    other_core = {"shard": s + 1 - 2 * core}
    wide = gl.shape[0] // 2
    span = wide // SIDE
    tall = from_y.shape[1]
    near = pl.ds(pl.multiple_of(core * wide, wide), wide)
    far = pl.ds(pl.multiple_of((1 - core) * wide, wide), wide)
    pairs = [
        (factor_basis, basis),
        (gate_anchor.at[far], ga.at[far]),
        (gate_local.at[0, far], gl.at[far]),
        (gate_anchor.at[near], ga.at[near]),
        (gate_local.at[0, near], gl.at[near]),
    ]
    loads = [pltpu.make_async_copy(src, dst, load_sem.at[i]) for i, (src, dst) in enumerate(pairs)]
    for load in loads:
        load.start()
    meet([other_core, along_x(1), along_x(3)] + [along_y(d) for d in range(1, SIDE)])

    def factor(start, target):
        def block(i, carry):
            rows = pl.ds(pl.multiple_of(start + i * span, span), span)
            diff = ga[rows, :] - gl[rows, :]
            target[i] = lax.dot_general(
                basis[...], diff, (((1,), (1,)), ((), ())), precision=HIGHEST, preferred_element_type=jnp.float32
            )
            return carry

        lax.fori_loop(0, SIDE, block, 0)

    for load in loads[:3]:
        load.wait()
    factor((1 - core) * wide, away)
    core_copy = remote(away, from_core, core_send, core_recv, other_core)
    core_copy.start()
    for load in loads[3:5]:
        load.wait()
    factor(core * wide, home)
    out[tall:, :] = jnp.zeros((8, span), jnp.float32)
    out[tall : tall + 2, 0 : norm_local.shape[2]] = norm_local[0]
    out[tall + 2 : tall + 3, 0 : norm_local.shape[2]] = norm_moment[...]
    core_copy.wait_recv()
    rank = row.shape[0]
    top, low = pl.ds(0, rank // 2), pl.ds(rank // 2, rank // 2)
    up, across, down = (x + 1) % SIDE, (x + 2) % SIDE, (x + 3) % SIDE

    def send_x(i, src, dst, d):
        copy = remote(src, dst, x_send.at[i], x_recv.at[i], along_x(d))
        copy.start()
        return copy

    home[across] = home[across] + from_core[across]
    x_copies = [
        send_x(0, home.at[across, top], via.at[0], 1),
        send_x(1, home.at[across, low], via.at[1], 3),
    ]
    home[up] = home[up] + from_core[up]
    x_copies.append(send_x(2, home.at[up, low], from_x.at[0, low], 1))
    home[down] = home[down] + from_core[down]
    x_copies.append(send_x(3, home.at[down, top], from_x.at[1, top], 3))
    row[...] = home[x] + from_core[x]
    x_copies[0].wait_recv()
    home[up, top, :] = home[up, top, :] + via[0]
    x_copies.append(send_x(4, home.at[up, top], from_x.at[0, top], 1))
    x_copies[1].wait_recv()
    home[down, low, :] = home[down, low, :] + via[1]
    x_copies.append(send_x(5, home.at[down, low], from_x.at[1, low], 3))
    for copy in x_copies[2:]:
        copy.wait_recv()
    row[...] = row[...] + (from_x[0] + from_x[1])
    y_copies = []
    for d in (2, 1, 3):
        rows = pl.ds(pl.multiple_of(((y + d) % SIDE) * tall, tall), tall)
        y_copies.append(remote(row.at[rows], from_y.at[d - 1], y_send.at[d - 1], y_recv.at[d - 1], along_y(d)))
        y_copies[-1].start()
    kept = pl.ds(pl.multiple_of(y * tall, tall), tall)
    for copy in y_copies:
        copy.wait_recv()
    out[0:tall, :] = (row[kept, :] + from_y[0]) + (from_y[1] + from_y[2])
    for copy in [core_copy] + x_copies + y_copies:
        copy.wait_send()


def gather_factors(
    own, peer, norm_anchor, out, new_norm_anchor, new_norm_moment,
    whole, core_send, core_recv, x_send, x_recv, y_send, y_recv,
):
    g = lax.axis_index("group")
    s = lax.axis_index("shard")
    x, y, core = s // (2 * SIDE), (s // 2) % SIDE, s % 2
    along_x, along_y = ring(s, True), ring(s, False)
    other_core = {"shard": s + 1 - 2 * core}
    tall = whole.shape[1] // SIDE
    meet([other_core] + [along_x(d) for d in range(1, SIDE)] + [along_y(d) for d in range(1, SIDE)])
    slot = core * SIDE + x
    kept = pl.ds(pl.multiple_of(y * tall, tall), tall)
    whole[slot, kept, :] = (own[0:tall, :] + peer[0:tall, :]) * (1.0 / groups)
    y_back = []
    for d in (2, 1, 3):
        here = whole.at[slot, kept]
        y_back.append(remote(here, here, y_send.at[d - 1], y_recv.at[d - 1], along_y(d)))
        y_back[-1].start()
    lanes = norm_anchor.shape[1]
    ours = own[tall : tall + 8, 0:lanes]
    theirs = peer[tall : tall + 8, 0:lanes]
    norm_delta = norm_anchor[...] - (ours[0:2] + theirs[0:2]) * (1.0 / groups)
    picked = lax.broadcasted_iota(jnp.int32, norm_anchor.shape, 0) == g
    norm_next = momentum * jnp.where(picked, ours[2:3], theirs[2:3]) + norm_delta
    new_norm_anchor[...] = norm_anchor[...] - outer_rate * (norm_delta + momentum * norm_next)
    new_norm_moment[...] = jnp.where(g == 0, norm_next[0:1], norm_next[1:2])
    for copy in y_back:
        copy.wait_recv()
    x_back = []
    for d in (2, 1, 3):
        here = whole.at[slot]
        x_back.append(remote(here, here, x_send.at[d - 1], x_recv.at[d - 1], along_x(d)))
        x_back[-1].start()
    for copy in x_back:
        copy.wait_recv()
    half = whole.at[pl.ds(pl.multiple_of(core * SIDE, SIDE), SIDE)]
    core_back = remote(half, half, core_send, core_recv, other_core)
    core_back.start()
    core_back.wait_recv()

    def move(i, carry):
        out[i] = whole[i]
        return carry

    lax.fori_loop(0, 2 * SIDE, move, 0)
    for copy in y_back + x_back + [core_back]:
        copy.wait_send()


def rebuild(
    gate_anchor, gate_moment, factor_basis, whole, norm_a, norm_m,
    new_anchor, new_moment, new_norm_anchor, new_norm_moment, ga, gm, store_sem,
):
    blocks = whole.shape[0]
    span = whole.shape[2]
    stores = []
    for i in range(blocks):
        rows = pl.ds(i * span, span)
        stores.append(pltpu.make_async_copy(ga.at[rows], new_anchor.at[rows], store_sem.at[2 * i]))
        stores.append(pltpu.make_async_copy(gm.at[rows], new_moment.at[rows], store_sem.at[2 * i + 1]))
    new_norm_anchor[...] = norm_a[...]
    new_norm_moment[...] = norm_m[...]
    for i in range(blocks):
        rows = pl.ds(i * span, span)
        delta = lax.dot_general(
            whole[i], factor_basis[...], (((0,), (0,)), ((), ())), precision=HIGHEST,
            preferred_element_type=jnp.float32,
        )
        moment = momentum * gate_moment[rows, :] + delta
        gm[rows, :] = moment
        ga[rows, :] = gate_anchor[rows, :] - outer_rate * (delta + momentum * moment)
        stores[2 * i].start()
        stores[2 * i + 1].start()
    for store in stores:
        store.wait()


def own_half(
    down_anchor, down_moment, raw, peer, down_local, part,
    new_anchor, new_moment, base, da, dm, dl, pr, load_sem, store_sem,
):
    half = part.shape[0]
    g = lax.axis_index("group")
    mine = pl.ds(pl.multiple_of(g * half, half), half)
    pairs = [
        (down_anchor, da),
        (down_moment, dm),
        (down_local.at[0, mine], dl),
        (peer, pr),
    ]
    loads = [pltpu.make_async_copy(src, dst, load_sem.at[i]) for i, (src, dst) in enumerate(pairs)]
    for load in loads:
        load.start()
    for load in loads:
        load.wait()

    def block(i, carry):
        rows = pl.ds(pl.multiple_of(i * 16, 16), 16)
        own = pl.ds(pl.multiple_of(g * half + i * 16, 16), 16)
        anchor = da[own, :]
        dm[rows, :] = momentum * dm[rows, :] + (anchor - (dl[rows, :] + pr[rows, :]) * (1.0 / groups))
        da[own, :] = (anchor_weight * anchor + local_weight * pr[rows, :]) + part[rows, :]
        far = pl.ds(pl.multiple_of((1 - g) * half + i * 16, 16), 16)
        base[rows, :] = anchor_weight * da[far, :] + local_weight * raw[rows, :]
        return carry

    lax.fori_loop(0, half // 16, block, 0)
    stores = [
        pltpu.make_async_copy(da.at[mine], new_anchor.at[mine], store_sem.at[0]),
        pltpu.make_async_copy(dm, new_moment, store_sem.at[1]),
    ]
    for store in stores:
        store.start()
    for store in stores:
        store.wait()


def other_half(given, base, peer, new_anchor, result, sem):
    del given
    half = base.shape[0]
    chunks = sem.shape[0]
    step = half // chunks
    g = lax.axis_index("group")
    stores = []
    for c in range(chunks):
        def block(i, carry):
            rows = pl.ds(pl.multiple_of(c * step + i * 8, 8), 8)
            result[rows, :] = base[rows, :] + peer[rows, :]
            return carry

        lax.fori_loop(0, step // 8, block, 0)
        rows = pl.ds(c * step, step)
        far = pl.ds(pl.multiple_of((1 - g) * half + c * step, step), step)
        stores.append(pltpu.make_async_copy(result.at[rows], new_anchor.at[far], sem.at[c]))
        stores[-1].start()
    for store in stores:
        store.wait()


def body(*args):
    (down_anchor, down_local, down_moment, norm_anchor, norm_local, norm_moment, gate_anchor, gate_local, gate_moment,
     factor_basis) = args
    f32 = jnp.float32
    half, width = down_moment.shape
    rank, depth = factor_basis.shape
    hidden = gate_anchor.shape[0]
    wide = hidden // 2
    span = wide // SIDE
    tall = rank // SIDE
    anywhere = pl.BlockSpec(memory_space=pl.ANY)
    vmem = pl.BlockSpec(memory_space=pltpu.VMEM)
    dma = pltpu.SemaphoreType.DMA
    V = lambda *shape: pltpu.VMEM(shape, f32)
    S = lambda a: jax.ShapeDtypeStruct(a.shape, f32)
    swap = [(0, 1), (1, 0)]

    def cost(us):
        return pl.CostEstimate(flops=0, bytes_accessed=int(us * 3.5e6), transcendentals=0)

    def params(mib, **more):
        return pltpu.CompilerParams(vmem_limit_bytes=mib << 20, **more)

    raw = pl.pallas_call(
        take_raw, out_shape=V(half, width), in_specs=[pl.BlockSpec(memory_space=pltpu.HBM)], out_specs=vmem, scratch_shapes=[dma],
        compiler_params=params(60), cost_estimate=cost(1),
    )(down_local)
    peer_raw = lax.ppermute(raw, "group", swap)
    part = pl.pallas_call(
        combine, out_shape=V(half, width), in_specs=[anywhere] * 2 + [vmem], out_specs=vmem,
        scratch_shapes=[V(half, width), V(half, width), dma((2,))], compiler_params=params(8), cost_estimate=cost(2),
    )(down_local, down_moment, raw)
    own = pl.pallas_call(
        reduce_factors,
        out_shape=V(tall + 8, span),
        in_specs=[anywhere] * 2 + [vmem] * 3,
        out_specs=vmem,
        scratch_shapes=[
            V(hidden, depth), V(hidden, depth), V(rank, depth), V(SIDE, rank, span), V(SIDE, rank, span),
            V(SIDE, rank, span), V(2, rank, span), V(2, rank // 2, span), V(rank, span), V(SIDE - 1, tall, span),
            dma((5,)), dma, dma, dma((6,)), dma((6,)), dma((3,)), dma((3,)),
        ],
        compiler_params=params(16, collective_id=0, has_side_effects=True), cost_estimate=cost(20),
    )(gate_anchor, gate_local, factor_basis, norm_local, norm_moment)
    peer = lax.ppermute(own, "group", swap)
    peer, peer_raw, part = lax.optimization_barrier((peer, peer_raw, part))
    peer_part = lax.ppermute(part, "group", swap)
    whole, norm_a, norm_m = pl.pallas_call(
        gather_factors,
        out_shape=[V(2 * SIDE, rank, span), V(*norm_anchor.shape), V(*norm_moment.shape)],
        in_specs=[vmem] * 3,
        out_specs=[vmem] * 3,
        scratch_shapes=[V(2 * SIDE, rank, span), dma, dma, dma((3,)), dma((3,)), dma((3,)), dma((3,))],
        compiler_params=params(8, collective_id=1, has_side_effects=True), cost_estimate=cost(15),
    )(own, peer, norm_anchor)
    new_gate_anchor, new_gate_moment, new_norm_anchor, new_norm_moment = pl.pallas_call(
        rebuild,
        out_shape=[S(gate_anchor), S(gate_moment), S(norm_anchor), S(norm_moment)],
        in_specs=[vmem] * 6,
        out_specs=[anywhere] * 2 + [vmem] * 2,
        scratch_shapes=[V(hidden, depth), V(hidden, depth), dma((4 * SIDE,))],
        compiler_params=params(16), cost_estimate=cost(5),
    )(gate_anchor, gate_moment, factor_basis, whole, norm_a, norm_m)
    peer_raw, _ = lax.optimization_barrier((peer_raw, whole))
    anchor, new_down_moment, base = pl.pallas_call(
        own_half,
        out_shape=[S(down_anchor), S(down_moment), V(half, width)],
        in_specs=[anywhere] * 2 + [vmem, anywhere, anywhere, vmem],
        out_specs=[anywhere] * 2 + [vmem],
        scratch_shapes=[V(2 * half, width)] + [V(half, width)] * 3 + [dma((4,)), dma((2,))],
        compiler_params=params(16), cost_estimate=cost(4),
    )(down_anchor, down_moment, raw, peer_raw, down_local, part)
    new_down_anchor = pl.pallas_call(
        other_half,
        out_shape=S(down_anchor),
        in_specs=[anywhere, vmem, vmem],
        out_specs=anywhere,
        input_output_aliases={0: 0},
        scratch_shapes=[V(half, width), dma((4,))],
        compiler_params=params(8), cost_estimate=cost(1),
    )(anchor, base, peer_part)
    return new_down_anchor, new_down_moment, new_norm_anchor, new_norm_moment, new_gate_anchor, new_gate_moment


def solution(mesh):
    placed = (
        P("shard", "tensor"),
        P("group", "shard", "tensor"),
        P(("shard", "group"), "tensor"),
        P(None, ("shard", "tensor")),
        P("group", None, ("shard", "tensor")),
        P("group", ("shard", "tensor")),
        P("tensor", "shard"),
        P("group", "tensor", "shard"),
        P("tensor", "shard"),
        P(None, "shard"),
    )
    return jax.shard_map(
        body,
        mesh=mesh,
        in_specs=placed,
        out_specs=(
            P("shard", "tensor"),
            P(("shard", "group"), "tensor"),
            P(None, ("shard", "tensor")),
            P("group", ("shard", "tensor")),
            P("tensor", "shard"),
            P("tensor", "shard"),
        ),
        check_vma=False,
    )
```
